256 devices in a mesh: vp: 128 (over y, x, z), op: 2 (over core).
Axes of the slice: x: 4, y: 4, z: 8, core: 2. Of those that a mesh axis runs over, the one named last changes fastest.
Arguments:
- multipliers: bfloat16 [2048, 131072], P('op', 'vp'), may hold values from -6 to 6
- integrals: bfloat16 [131072, 1024], P('vp'), may hold values from -0.0625 to 0.0625
- amplitudes: bfloat16 [2048, 131072], P('op', 'vp'), may hold values from -0.09375 to 0.09375
- slab_multipliers: bfloat16 [1024, 2048], P('vp', 'op'), may hold values from -6 to 6
- slab_amplitudes: bfloat16 [1024, 2048], P('vp', 'op'), may hold values from -0.09375 to 0.09375
- residual_rest: bfloat16 [1024, 2048], P('vp', 'op'), may hold values from -6 to 6
- occupied_energy: bfloat16 [2048], P('op'), may hold values from -2.5 to -0.5
- virtual_energy: bfloat16 [1024], P('vp'), may hold values from 1 to 4
Outputs:
- updated_multipliers: bfloat16 [1024, 2048], P('vp', 'op')
- pair_density: bfloat16 [1024, 131072], P('op', 'vp')
The draws below stay inside these ranges and needn't reach their ends.
All inputs are finite; a program needn't handle non-finite values.
Results may differ from the reference program's by a relative error of at most 0.004.
Values may be sent and summed in bfloat16 or wider, within the bound.
A program may use at most 64 MiB of HBM per device.

```python
import jax
import jax.numpy as jnp
from jax import lax

P_SIZE = 2048
Q = 131072
SLAB_PAIRS = 1024


def with_spikes(entries, stream_key, source, target, parts, factor):
    owner, partner = [(jnp.arange(entries.shape[dim]) // (entries.shape[dim] // parts)).reshape([-1 if axis == dim else 1 for axis in range(entries.ndim)]) for dim in (source, target)]
    chosen = jax.random.permutation(stream_key, parts)[partner]
    strong = (owner == chosen) | (owner == (partner + parts // 2) % parts)
    return jnp.where(strong, factor * entries, entries)


def block_levels(key, extent, pieces, smallest, top_value):
    def one(position, parts):
        draws = jax.random.uniform(jax.random.fold_in(jax.random.fold_in(key, 6), position), (parts,), jnp.float32, smallest / len(pieces), top_value / len(pieces))
        return jnp.repeat(jnp.exp(draws), extent[position] // parts).reshape((-1,) + (1,) * (len(extent) - position - 1))

    level = one(*pieces[0])
    for cut in pieces[1:]:
        level = level * one(*cut)
    return level


def centred(stream_key, dims, deviation, reach, cuts=(), held_as=jnp.bfloat16):
    gain = block_levels(stream_key, dims, cuts, -0.22, 0.18) if cuts else 1.0
    result = jax.random.normal(stream_key, dims, jnp.float32) * deviation * gain
    return jnp.minimum(jnp.maximum(result, -reach), reach).astype(held_as)


def heavy_noise(rng, shape, deviation, most, shards, heavy, held_as=jnp.bfloat16):
    drawn = deviation * jax.random.normal(rng, shape, jnp.float32)
    if shards:
        drawn = drawn * block_levels(rng, shape, shards, -0.22, 0.18)
    return jnp.clip(with_spikes(drawn, jax.random.fold_in(rng, 3), *heavy), -most, most).astype(held_as)


def setup_inputs(seed: int = 0) -> dict:
    seeds = jax.random.split(jax.random.key(seed), 9)
    multipliers = centred(seeds[0], (P_SIZE, Q), 1.0, 6.0, ((0, 2), (1, 128)))
    integrals = heavy_noise(seeds[1], (Q, SLAB_PAIRS), Q ** -0.5, 0.0625, ((0, 128),), (0, 1, 128, 5.5))
    amplitudes = centred(seeds[2], (P_SIZE, Q), (1.0 / (2 * P_SIZE) ** 0.5), 0.09375, ((0, 2), (1, 128)))
    slab_multipliers = centred(seeds[3], (SLAB_PAIRS, P_SIZE), 1.0, 6.0, ((0, 128), (1, 2)))
    slab_amplitudes = centred(seeds[4], (SLAB_PAIRS, P_SIZE), (1.0 / (2 * P_SIZE) ** 0.5), 0.09375, ((0, 128), (1, 2)))
    residual_rest = centred(seeds[5], (SLAB_PAIRS, P_SIZE), 1.0, 6.0, ((0, 128), (1, 2)))
    occupied_energy = jnp.clip(-2.5 + 2.0 * jax.random.uniform(seeds[6], (P_SIZE,), jnp.float32) ** block_levels(seeds[6], (P_SIZE,), ((0, 2),), -0.2, 0.2), -2.5, -0.5).astype(jnp.bfloat16)
    virtual_energy = jnp.clip(1.0 + 3.0 * jax.random.uniform(seeds[7], (SLAB_PAIRS,), jnp.float32) ** block_levels(seeds[7], (SLAB_PAIRS,), ((0, 128),), -0.2, 0.2), 1.0, 4.0).astype(jnp.bfloat16)
    return dict(multipliers=multipliers, integrals=integrals, amplitudes=amplitudes, slab_multipliers=slab_multipliers, slab_amplitudes=slab_amplitudes, residual_rest=residual_rest, occupied_energy=occupied_energy, virtual_energy=virtual_energy)


def reference(multipliers, integrals, amplitudes, slab_multipliers, slab_amplitudes, residual_rest, occupied_energy, virtual_energy):
    ladder = lax.dot_general(integrals, multipliers, (((0,), (1,)), ((), ())), preferred_element_type=jnp.float32)
    divisor = virtual_energy.astype(jnp.float32)[:, None] - occupied_energy.astype(jnp.float32)[None, :]
    renewed = slab_multipliers.astype(jnp.float32) + (ladder + residual_rest.astype(jnp.float32)) / divisor
    renewed = renewed.astype(jnp.bfloat16)
    density = jnp.dot(renewed, amplitudes, preferred_element_type=jnp.float32)
    density = density + jnp.dot(slab_amplitudes, multipliers, preferred_element_type=jnp.float32)
    return renewed, density.astype(jnp.bfloat16)
```

```python
import jax
import jax.numpy as jnp
from jax import lax
from jax.sharding import PartitionSpec as P


def renew_slab(current, ladder, rest, virtual, occupied):
    divisor = virtual.astype(jnp.float32)[:, None] - occupied.astype(jnp.float32)[None, :]
    renewed = current.astype(jnp.float32) + (ladder + rest.astype(jnp.float32)) / divisor
    return renewed.astype(jnp.bfloat16)


def local(
    multipliers,
    integrals,
    amplitudes,
    slab_multipliers,
    slab_amplitudes,
    residual_rest,
    occupied_energy,
    virtual_energy,
):
    every_amp = lax.all_gather(slab_amplitudes, "vp", axis=0, tiled=True)
    ladder = lax.psum_scatter(
        lax.dot_general(
            integrals, multipliers, (((0,), (1,)), ((), ())), preferred_element_type=jnp.float32
        ),
        "vp",
        scatter_dimension=0,
        tiled=True,
    )
    renewed = renew_slab(
        slab_multipliers, ladder, residual_rest, virtual_energy, occupied_energy
    )
    every_new = lax.all_gather(renewed, "vp", axis=0, tiled=True)
    first = jnp.dot(every_new, amplitudes, preferred_element_type=jnp.float32)
    density = lax.psum_scatter(
        first + jnp.dot(every_amp, multipliers, preferred_element_type=jnp.float32),
        "op",
        scatter_dimension=0,
        tiled=True,
    )
    return (renewed, density.astype(jnp.bfloat16))


def solution(mesh):
    placed = (
        P("op", "vp"),
        P("vp", None),
        P("op", "vp"),
        P("vp", "op"),
        P("vp", "op"),
        P("vp", "op"),
        P("op"),
        P("vp"),
    )
    return jax.shard_map(
        local, mesh=mesh, in_specs=placed, out_specs=(P("vp", "op"), P("op", "vp")), check_vma=False
    )
```

```python
import functools

import jax
import jax.numpy as jnp
from jax import lax
from jax.experimental import pallas as pl
from jax.experimental.pallas import tpu as pltpu
from jax.sharding import PartitionSpec as P

F32 = jnp.float32
BF16 = jnp.bfloat16


def kernel(
    dims,
    mul_hbm, int_hbm, amp_hbm, slab_ref, slab_amp_ref, rest_ref, div_ref,
    new_ref, den_ref,
    mul, integ, amp, lad, got1a, got1b, sum1, got2, sum2, got3,
    new_z, new_all, am_z, am_all, acc, swap_out, swap_in,
    load_sem,
    s1a, r1a, s1b, r1b, s2, r2, s3, r3,
    nz_s, nz_r, n2_s, n2_r, n3_s, n3_r,
    az_s, az_r, a2_s, a2_r, a3_s, a3_r,
    sw_s, sw_r,
):
    Y, X, Z = dims
    v = lax.axis_index("vp")
    c = lax.axis_index("op")
    y = v // (X * Z)
    x = lax.rem(v // Z, X)
    z = lax.rem(v, Z)
    B = 8 * Z
    W = lad.shape[-1]

    def peer_y(k):
        return lax.rem(y + k, Y)

    def peer_x(k):
        return lax.rem(x + k, X)

    def peer_z(k):
        return lax.rem(z + k, Z)

    def at_y(i):
        return {"vp": (i * X + x) * Z + z}

    def at_x(i):
        return {"vp": (y * X + i) * Z + z}

    def at_z(i):
        return {"vp": (y * X + x) * Z + i}

    other = {"op": 1 - c}

    def remote(src, dst, ss, rs, device):
        return pltpu.make_async_remote_copy(
            src_ref=src, dst_ref=dst, send_sem=ss, recv_sem=rs,
            device_id=device, device_id_type=pl.DeviceIdType.MESH,
        )

    load_m = pltpu.make_async_copy(mul_hbm, mul, load_sem.at[0])
    load_i = pltpu.make_async_copy(int_hbm, integ, load_sem.at[1])
    load_a = pltpu.make_async_copy(amp_hbm, amp, load_sem.at[2])
    load_m.start()
    load_i.start()
    load_a.start()

    barrier = pltpu.get_barrier_semaphore()
    greet = (
        [at_y(peer_y(k)) for k in range(1, Y)]
        + [at_x(peer_x(k)) for k in range(1, X)]
        + [at_z(peer_z(k)) for k in range(1, Z)]
        + [other]
    )
    for device in greet:
        pl.semaphore_signal(barrier, inc=1, device_id=device, device_id_type=pl.DeviceIdType.MESH)

    rows_z = pl.ds(pl.multiple_of(z * 8, 8), 8)
    am_z[rows_z, :] = slab_amp_ref[...].astype(F32)
    load_m.wait()
    load_i.wait()
    pl.semaphore_wait(barrier, len(greet))

    def spread_z(buf, ss, rs):
        out = []
        for k in range(1, Z):
            d = remote(
                buf.at[rows_z, :], buf.at[rows_z, :], ss.at[k - 1], rs.at[Z - 1 - k],
                at_z(peer_z(k)),
            )
            d.start()
            out.append(d)
        return out

    def spread_own(buf_z, full, ss2, rs2, ss3, rs3):
        out = []
        full[0, y, x] = buf_z[:, :W].astype(BF16)
        full[1, y, x] = buf_z[:, W:].astype(BF16)
        for k in range(1, Y):
            here = full.at[0, y, x]
            d = remote(here, here, ss2.at[0, k - 1], rs2.at[0, Y - 1 - k], at_y(peer_y(k)))
            d.start()
            out.append(d)
            here = full.at[1, y, x]
            d = remote(here, here, ss2.at[1, k - 1], rs2.at[1, X - 1 - k], at_x(peer_x(k)))
            d.start()
            out.append(d)
        for k in range(1, Y):
            here = full.at[0, y, x]
            d = remote(here, here, ss3.at[0, k - 1, 0], rs3.at[0, X - 1 - k, 0], at_x(peer_x(k)))
            d.start()
            out.append(d)
            here = full.at[1, y, x]
            d = remote(here, here, ss3.at[1, k - 1, 0], rs3.at[1, Y - 1 - k, 0], at_y(peer_y(k)))
            d.start()
            out.append(d)
        return out

    def spread_got(full, got2_d, ss3, rs3):
        out = []
        for i in range(Y - 1):
            got2_d[0][i].wait_recv()
            here = full.at[0, peer_y(i + 1), x]
            for k in range(1, X):
                d = remote(
                    here, here, ss3.at[0, k - 1, i + 1], rs3.at[0, X - 1 - k, i + 1],
                    at_x(peer_x(k)),
                )
                d.start()
                out.append(d)
            got2_d[1][i].wait_recv()
            here = full.at[1, y, peer_x(i + 1)]
            for k in range(1, Y):
                d = remote(
                    here, here, ss3.at[1, k - 1, i + 1], rs3.at[1, Y - 1 - k, i + 1],
                    at_y(peer_y(k)),
                )
                d.start()
                out.append(d)
        return out

    def arrivals_z(buf, ss, rs):
        out = []
        for i in range(Z - 1):
            rows = pl.ds(pl.multiple_of(peer_z(i + 1) * 8, 8), 8)
            out.append(remote(buf.at[rows, :], buf.at[rows, :], ss.at[i], rs.at[i], at_z(peer_z(i + 1))))
        return out

    def arrivals_2(full, ss, rs):
        a = []
        b = []
        for i in range(Y - 1):
            here = full.at[0, peer_y(i + 1), x]
            a.append(remote(here, here, ss.at[0, i], rs.at[0, i], at_y(peer_y(i + 1))))
        for i in range(X - 1):
            here = full.at[1, y, peer_x(i + 1)]
            b.append(remote(here, here, ss.at[1, i], rs.at[1, i], at_x(peer_x(i + 1))))
        return a, b

    def arrivals_3(full, ss, rs):
        out = []
        for j in range(Y):
            for i in range(X - 1):
                here = full.at[0, peer_y(j), peer_x(i + 1)]
                out.append(remote(here, here, ss.at[0, i, j], rs.at[0, i, j], at_x(peer_x(i + 1))))
                here = full.at[1, peer_y(i + 1), peer_x(j)]
                out.append(remote(here, here, ss.at[1, i, j], rs.at[1, i, j], at_y(peer_y(i + 1))))
        return out

    sent = []
    sent += spread_z(am_z, az_s, az_r)

    for n in range(Y):
        k = n + 1
        yb = peer_y(k)
        cols = pl.ds(pl.multiple_of(yb * (X * B), X * B), X * B)
        part = lax.dot_general(
            integ[:, cols], mul[...], (((0,), (1,)), ((), ())), preferred_element_type=F32
        )
        lad[0, yb] = part[:, :W].astype(BF16).reshape(X, B, W)
        lad[1, yb] = part[:, W:].astype(BF16).reshape(X, B, W)
        if k < Y:
            d = remote(lad.at[1, yb], got1b.at[Y - 1 - k], s1b.at[k - 1], r1b.at[Y - 1 - k], at_y(yb))
            d.start()
            sent.append(d)
        for kx in range(1, X):
            xb = peer_x(kx)
            d = remote(
                lad.at[0, yb, xb], got1a.at[X - 1 - kx, yb],
                s1a.at[kx - 1, n], r1a.at[X - 1 - kx, n], at_x(xb),
            )
            d.start()
            sent.append(d)

    for d in arrivals_z(am_z, az_s, az_r):
        d.wait_recv()
    sent += spread_own(am_z, am_all, a2_s, a2_r, a3_s, a3_r)

    for n in range(Y):
        k = n + 1
        yb = peer_y(k)
        for i in range(X - 1):
            remote(
                lad.at[0, yb, x], got1a.at[i, yb], s1a.at[i, n], r1a.at[i, n], at_x(peer_x(i + 1))
            ).wait_recv()
        total = lad[0, yb, x].astype(F32)
        for i in range(X - 1):
            total = total + got1a[i, yb].astype(F32)
        if k < Y:
            sum1[0, n] = total.astype(BF16)
            d = remote(sum1.at[0, n], got2.at[0, Y - 1 - k], s2.at[0, n], r2.at[0, Y - 1 - k], at_y(yb))
            d.start()
            sent.append(d)
        else:
            sum2[:, :W] = total
    for i in range(Y - 1):
        remote(
            lad.at[1, y], got1b.at[i], s1b.at[i], r1b.at[i], at_y(peer_y(i + 1))
        ).wait_recv()
    for n in range(X):
        k = n + 1
        xb = peer_x(k)
        total = lad[1, y, xb].astype(F32)
        for i in range(Y - 1):
            total = total + got1b[i, xb].astype(F32)
        if k < X:
            sum1[1, n] = total.astype(BF16)
            d = remote(sum1.at[1, n], got2.at[1, X - 1 - k], s2.at[1, n], r2.at[1, X - 1 - k], at_x(xb))
            d.start()
            sent.append(d)
        else:
            sum2[:, W:] = total

    for h in range(2):
        cols = slice(h * W, (h + 1) * W)
        for i in range(got2.shape[1]):
            device = at_y(peer_y(i + 1)) if h == 0 else at_x(peer_x(i + 1))
            remote(sum1.at[h, i], got2.at[h, i], s2.at[h, i], r2.at[h, i], device).wait_recv()
        total = sum2[:, cols]
        for i in range(got2.shape[1]):
            total = total + got2[h, i].astype(F32)
        sum2[:, cols] = total
    for k in range(1, Z):
        zb = peer_z(k)
        rows = pl.ds(pl.multiple_of(zb * 8, 8), 8)
        d = remote(sum2.at[rows, :], got3.at[Z - 1 - k], s3.at[k - 1], r3.at[Z - 1 - k], at_z(zb))
        d.start()
        sent.append(d)

    for i in range(Z - 1):
        remote(
            sum2.at[rows_z, :], got3.at[i], s3.at[i], r3.at[i], at_z(peer_z(i + 1))
        ).wait_recv()
    ladder = sum2[rows_z, :]
    for i in range(Z - 1):
        ladder = ladder + got3[i]
    renewed = slab_ref[...].astype(F32) + (ladder + rest_ref[...].astype(F32)) / div_ref[...]
    renewed = renewed.astype(BF16)
    new_ref[...] = renewed
    new_z[rows_z, :] = renewed.astype(F32)
    sent += spread_z(new_z, nz_s, nz_r)

    sent += spread_got(am_all, arrivals_2(am_all, a2_s, a2_r), a3_s, a3_r)

    for d in arrivals_z(new_z, nz_s, nz_r):
        d.wait_recv()
    sent += spread_own(new_z, new_all, n2_s, n2_r, n3_s, n3_r)
    sent += spread_got(new_all, arrivals_2(new_all, n2_s, n2_r), n3_s, n3_r)

    for d in arrivals_3(am_all, a3_s, a3_r):
        d.wait_recv()
    R = X * B
    first = 1 - c

    def block_of(t):
        return jnp.where(t < Y // 2, first * (Y // 2) + t, c * (Y // 2) + t - Y // 2)

    @pl.loop(0, Y)
    def _(t):
        yb = block_of(t)
        acc[t] = jnp.dot(
            am_all[0, yb].reshape(R, W), mul[:W, :], preferred_element_type=F32
        ) + jnp.dot(am_all[1, yb].reshape(R, W), mul[W:, :], preferred_element_type=F32)

    load_a.wait()
    for d in arrivals_3(new_all, n3_s, n3_r):
        d.wait_recv()

    def density(t):
        yb = block_of(t)
        return (
            acc[t]
            + jnp.dot(new_all[0, yb].reshape(R, W), amp[:W, :], preferred_element_type=F32)
            + jnp.dot(new_all[1, yb].reshape(R, W), amp[W:, :], preferred_element_type=F32)
        )

    swaps = []
    for t in range(Y // 2):
        swap_out[t] = density(t).astype(swap_out.dtype)
        d = remote(swap_out.at[t], swap_in.at[t], sw_s.at[t], sw_r.at[t], other)
        d.start()
        swaps.append(d)
    for t in range(Y // 2):
        acc[Y // 2 + t] = density(Y // 2 + t)
    for t in range(Y // 2):
        swaps[t].wait_recv()
        den_ref[pl.ds(t * R, R), :] = (acc[Y // 2 + t] + swap_in[t].astype(F32)).astype(BF16)
    for d in sent + swaps:
        d.wait_send()


def local(dims, mul, integ, amp, slab, slab_amp, rest, occupied, virtual):
    Y, X, Z = dims
    B = 8 * Z
    R = Y * X * B
    p, q = mul.shape
    W = p // 2
    divisor = virtual.astype(F32)[:, None] - occupied.astype(F32)[None, :]
    dma = pltpu.SemaphoreType.DMA
    vmem = pl.BlockSpec(memory_space=pltpu.VMEM)
    hbm = pl.BlockSpec(memory_space=pl.ANY)
    gather_sems = [
        dma((Z - 1,)), dma((Z - 1,)),
        dma((2, Y - 1)), dma((2, Y - 1)),
        dma((2, Y - 1, Y)), dma((2, Y - 1, Y)),
    ]
    scratch = [
        pltpu.VMEM((p, q), BF16),
        pltpu.VMEM((q, R), BF16),
        pltpu.VMEM((p, q), BF16),
        pltpu.VMEM((2, Y, X, B, W), BF16),
        pltpu.VMEM((X - 1, Y, B, W), BF16),
        pltpu.VMEM((Y - 1, X, B, W), BF16),
        pltpu.VMEM((2, Y - 1, B, W), BF16),
        pltpu.VMEM((2, Y - 1, B, W), BF16),
        pltpu.VMEM((B, p), F32),
        pltpu.VMEM((Z - 1, 8, p), F32),
        pltpu.VMEM((B, p), F32),
        pltpu.VMEM((2, Y, X, B, W), BF16),
        pltpu.VMEM((B, p), F32),
        pltpu.VMEM((2, Y, X, B, W), BF16),
        pltpu.VMEM((Y, R // Y, q), F32),
        pltpu.VMEM((Y // 2, R // Y, q), BF16),
        pltpu.VMEM((Y // 2, R // Y, q), BF16),
        dma((3,)),
        dma((X - 1, Y)), dma((X - 1, Y)),
        dma((Y - 1,)), dma((Y - 1,)),
        dma((2, Y - 1)), dma((2, Y - 1)),
        dma((Z - 1,)), dma((Z - 1,)),
        *gather_sems,
        *gather_sems,
        dma((Y // 2,)), dma((Y // 2,)),
    ]
    return pl.pallas_call(
        functools.partial(kernel, dims),
        out_shape=(
            jax.ShapeDtypeStruct((8, p), BF16),
            jax.ShapeDtypeStruct((R // 2, q), BF16),
        ),
        in_specs=[hbm, hbm, hbm, vmem, vmem, vmem, vmem],
        out_specs=(vmem, vmem),
        scratch_shapes=scratch,
        compiler_params=pltpu.CompilerParams(
            collective_id=0, has_side_effects=True, vmem_limit_bytes=50 * 1024 * 1024
        ),
        name="ladder_step",
    )(mul, integ, amp, slab, slab_amp, rest, divisor)


def solution(mesh, dims=(4, 4, 8)):
    placed = (
        P("op", "vp"),
        P("vp", None),
        P("op", "vp"),
        P("vp", "op"),
        P("vp", "op"),
        P("vp", "op"),
        P("op"),
        P("vp"),
    )
    return jax.shard_map(
        functools.partial(local, dims), mesh=mesh, in_specs=placed,
        out_specs=(P("vp", "op"), P("op", "vp")), check_vma=False,
    )
```

```python
import functools

import jax
import jax.numpy as jnp
from jax import lax
from jax.experimental import pallas as pl
from jax.experimental.pallas import tpu as pltpu
from jax.sharding import PartitionSpec as P

F32 = jnp.float32
BF16 = jnp.bfloat16
CHUNKS = 4


def kernel(
    dims,
    mul_hbm, int_hbm, amp_hbm, slab_hbm, slab_amp_hbm, rest_hbm, occ_hbm, virt_hbm,
    new_ref, den_ref,
    mul, integ, amp, slab, rest, occ, virt,
    lad, got1, sum1, got2, own3, sum2, got3, new_z, new_all, am_all, acc, swap_out, swap_in,
    load_sem, s1, r1, s2, r2, s3, r3, nz_s, nz_r, n2_s, n2_r, n3_s, n3_r,
    ax_s, ax_r, ay_s, ay_r, az_s, az_r, sw_s, sw_r,
):
    Y, X, Z = dims
    N = Y
    v = lax.axis_index("vp")
    c = lax.axis_index("op")
    y = v // (X * Z)
    x = lax.rem(v // Z, X)
    z = lax.rem(v, Z)
    B = 8 * Z
    R = X * B
    W = lad.shape[-1]
    chunks = lad.shape[0] // 2

    def near(axis, k):
        return lax.rem((y, x, z)[axis] + k, dims[axis])

    def at(axis, i):
        if axis == 0:
            return {"vp": (i * X + x) * Z + z}
        if axis == 1:
            return {"vp": (y * X + i) * Z + z}
        return {"vp": (y * X + x) * Z + i}

    other = {"op": 1 - c}
    sent = []

    def remote(src, dst, ss, rs, device):
        return pltpu.make_async_remote_copy(
            src_ref=src, dst_ref=dst, send_sem=ss, recv_sem=rs,
            device_id=device, device_id_type=pl.DeviceIdType.MESH,
        )

    def send(src, dst, ss, rs, device):
        d = remote(src, dst, ss, rs, device)
        d.start()
        sent.append(d)

    def arrived(ref, ss, rs, device):
        remote(ref, ref, ss, rs, device).wait_recv()

    def post(src, dst, ss, rs, device):
        remote(src, dst, ss, rs, device).start()

    def landed(bulk, ss, rs):
        remote(bulk, bulk, ss, rs, other).wait_recv()

    def left(bulk, ss, rs):
        remote(bulk, bulk, ss, rs, other).wait_send()

    loads = [
        pltpu.make_async_copy(src, dst, load_sem.at[i])
        for i, (src, dst) in enumerate([
            (slab_amp_hbm, am_all.at[z, y, x]), (int_hbm, integ), (mul_hbm, mul),
            (slab_hbm, slab), (rest_hbm, rest), (occ_hbm, occ), (virt_hbm, virt), (amp_hbm, amp),
        ])
    ]
    for d in loads:
        d.start()

    barrier = pltpu.get_barrier_semaphore()
    greet = [at(a, near(a, k)) for a in range(3) for k in range(1, dims[a])] + [other]
    for device in greet:
        pl.semaphore_signal(barrier, inc=1, device_id=device, device_id_type=pl.DeviceIdType.MESH)
    def amp_own():
        mine = am_all.at[z, y, x]
        for k in range(1, X):
            send(mine, mine, ax_s.at[k - 1], ax_r.at[X - 1 - k], at(1, near(1, k)))

    def amp_rows():
        for i in range(X - 1):
            arrived(am_all.at[z, y, near(1, i + 1)], ax_s.at[i], ax_r.at[i], at(1, near(1, i + 1)))
        row = am_all.at[z, y]
        for k in range(1, Y):
            send(row, row, ay_s.at[k - 1], ay_r.at[Y - 1 - k], at(0, near(0, k)))

    H = Z // 2

    def ring_piece(side, step):
        block = near(2, Z - (step - 1)) if side == 0 else near(2, step - 1)
        if step < H:
            return am_all.at[block]
        return am_all.at[block, pl.ds(side * (Y // 2), Y // 2)]

    def ring_landed(side, step):
        block = near(2, Z - step) if side == 0 else near(2, step)
        if step < H:
            return am_all.at[block]
        return am_all.at[block, pl.ds(side * (Y // 2), Y // 2)]

    def ring_wait(step):
        for side in range(2):
            arrived(
                ring_landed(side, step), az_s.at[side, step - 1], az_r.at[side, step - 1],
                at(2, near(2, 1 if side == 0 else Z - 1)),
            )

    def ring_step(step):
        if step == 1:
            for i in range(Y - 1):
                arrived(am_all.at[z, near(0, i + 1)], ay_s.at[i], ay_r.at[i], at(0, near(0, i + 1)))
        else:
            ring_wait(step - 1)
        for side in range(2):
            piece = ring_piece(side, step)
            send(
                piece, piece, az_s.at[side, step - 1], az_r.at[side, step - 1],
                at(2, near(2, 1 if side == 0 else Z - 1)),
            )

    def axes(s):
        return (1, 0) if s % 2 == 0 else (0, 1)

    def ladder(part):
        streams = range(part * chunks, (part + 1) * chunks)
        lo = part * chunks * W
        for n in range(N):
            tile = lax.dot_general(
                integ[:, n * R:(n + 1) * R], mul[lo:lo + chunks * W, :],
                (((0,), (1,)), ((), ())), preferred_element_type=F32,
            )
            for s in streams:
                piece = tile[:, s * W - lo:(s + 1) * W - lo].astype(BF16).reshape(X, B, W)
                if s % 2 == 0:
                    lad[s, :, n] = piece
                else:
                    lad[s, n] = piece

    def ladder_send(chunk):
        for k in (2, 1, 3) if N == 4 else range(1, N):
            for s in (2 * chunk, 2 * chunk + 1):
                one = axes(s)[0]
                j = near(one, k)
                post(lad.at[s, j], got1.at[s, N - 1 - k], s1.at[chunk], r1.at[chunk], at(one, j))

    def sum_first(chunk):
        landed(got1.at[pl.ds(2 * chunk, 2)], s1.at[chunk], r1.at[chunk])
        for s in (2 * chunk + 1, 2 * chunk):
            one, two = axes(s)
            me = (y, x)[one]
            for n in range(N):
                k = n + 1
                b = near(two, k)
                total = lad[s, me, b].astype(F32)
                for i in range(N - 1):
                    total = total + got1[s, i, b].astype(F32)
                if k < N:
                    sum1[s, n] = total.astype(BF16)
                    post(
                        sum1.at[s, n], got2.at[s, N - 1 - k], s2.at[chunk], r2.at[chunk], at(two, b)
                    )
                else:
                    own3[chunk, :, (s % 2) * W:(s % 2 + 1) * W] = total

    def sum_second(chunk):
        landed(got2.at[pl.ds(2 * chunk, 2)], s2.at[chunk], r2.at[chunk])
        for o in range(2):
            s = 2 * chunk + o
            two = axes(s)[1]
            cols = slice(o * W, (o + 1) * W)
            total = own3[chunk, :, cols]
            for i in range(N - 1):
                total = total + got2[s, i].astype(F32)
            own3[chunk, :, cols] = total
            sum2[chunk, :, :, cols] = total.reshape(Z, 8, W).astype(BF16)
        for k in range(1, Z):
            zb = near(2, k)
            post(
                sum2.at[chunk, zb], got3.at[chunk, Z - 1 - k], s3.at[chunk], r3.at[chunk], at(2, zb)
            )

    def renew(chunk):
        cols = slice(chunk * 2 * W, (chunk + 1) * 2 * W)
        landed(got3.at[chunk], s3.at[chunk], r3.at[chunk])
        total = own3[chunk, pl.ds(pl.multiple_of(z * 8, 8), 8), :]
        for i in range(Z - 1):
            total = total + got3[chunk, i].astype(F32)
        row = lax.broadcasted_iota(jnp.int32, (8, 8), 0)
        col = lax.broadcasted_iota(jnp.int32, (8, 8), 1)
        energy = jnp.broadcast_to(virt[...].astype(F32).reshape(1, 8), (8, 8))
        energy = jnp.sum(jnp.where(row == col, energy, 0.0), axis=1, keepdims=True)
        divisor = energy - occ[cols].astype(F32).reshape(1, 2 * W)
        renewed = slab[:, cols].astype(F32) + (total + rest[:, cols].astype(F32)) / divisor
        renewed = renewed.astype(BF16)
        new_ref[:, cols] = renewed
        new_z[chunk, z] = renewed
        here = new_z.at[chunk, z]
        for k in range(1, Z):
            post(here, here, nz_s.at[chunk], nz_r.at[chunk], at(2, near(2, k)))

    def spread_own(chunk):
        landed(got3.at[chunk], nz_s.at[chunk], nz_r.at[chunk])
        whole = new_z[chunk].astype(F32).reshape(B, 2 * W).astype(BF16)
        new_all[y, x, :, chunk * 2 * W:(chunk + 1) * 2 * W] = whole
        for k in (2, 1, 3) if N == 4 else range(1, N):
            for s in (2 * chunk, 2 * chunk + 1):
                two = axes(s)[1]
                here = new_all.at[y, x, :, pl.ds(s * W, W)]
                post(here, here, n2_s.at[chunk], n2_r.at[chunk], at(two, near(two, k)))

    def spread_got(chunk):
        landed(got2.at[pl.ds(2 * chunk, 2)], n2_s.at[chunk], n2_r.at[chunk])
        for k in (2, 1, 3) if N == 4 else range(1, N):
            for s in (2 * chunk, 2 * chunk + 1):
                one = axes(s)[0]
                cols = pl.ds(s * W, W)
                here = new_all.at[:, x, :, cols] if s % 2 == 0 else new_all.at[y, :, :, cols]
                post(here, here, n3_s.at[chunk], n3_r.at[chunk], at(one, near(one, k)))

    def spread_wait(chunk):
        landed(got1.at[pl.ds(2 * chunk, 2)], n3_s.at[chunk], n3_r.at[chunk])

    def all_left(chunk):
        pair = pl.ds(2 * chunk, 2)
        left(got1.at[pair], s1.at[chunk], r1.at[chunk])
        left(got2.at[pair], s2.at[chunk], r2.at[chunk])
        left(got3.at[chunk], s3.at[chunk], r3.at[chunk])
        left(got3.at[chunk], nz_s.at[chunk], nz_r.at[chunk])
        left(got2.at[pair], n2_s.at[chunk], n2_r.at[chunk])

    def amp_part(zb):
        rows = am_all[zb].astype(F32).reshape(Y * X * 8, mul.shape[0]).astype(BF16)
        acc[:, :, zb] = jnp.dot(rows, mul[...], preferred_element_type=F32).reshape(Y, X, 8, acc.shape[-1])

    K = mul.shape[0] // 2

    def product(half, yb):
        left = new_all[yb, :, :, half * K:(half + 1) * K].reshape(R, K)
        return jnp.dot(left, amp[half * K:(half + 1) * K, :], preferred_element_type=F32)

    loads[1].wait()
    loads[2].wait()
    ladder(0)
    loads[0].wait()
    pl.semaphore_wait(barrier, len(greet))
    amp_own()
    ladder_send(0)
    ladder_send(1)
    ladder(1)
    amp_rows()
    sum_first(0)
    ladder_send(2)
    for d in loads[3:]:
        d.wait()
    sum_second(0)
    sum_first(1)
    ladder_send(3)
    ring_step(1)
    renew(0)
    sum_second(1)
    sum_first(2)
    amp_part(z)
    spread_own(0)
    renew(1)
    sum_second(2)
    sum_first(3)
    ring_step(2)
    spread_got(0)
    spread_own(1)
    renew(2)
    sum_second(3)
    amp_part(near(2, 1))
    amp_part(near(2, Z - 1))
    spread_got(1)
    spread_own(2)
    renew(3)
    ring_step(3)
    spread_got(2)
    spread_own(3)
    amp_part(near(2, 2))
    amp_part(near(2, Z - 2))
    spread_got(3)
    ring_step(4)
    amp_part(near(2, 3))
    amp_part(near(2, Z - 3))
    ring_wait(4)
    amp_part(near(2, H))
    for chunk in range(chunks):
        all_left(chunk)
    for chunk in range(chunks // 2):
        spread_wait(chunk)

    @pl.loop(0, Y)
    def _(t):
        acc[t] = acc[t] + product(0, t).reshape(acc.shape[1:])

    for chunk in range(chunks // 2, chunks):
        spread_wait(chunk)
    swaps = []
    for t in range(Y // 2):
        yb = (1 - c) * (Y // 2) + t
        swap_out[t] = (acc[yb].reshape(R, acc.shape[-1]) + product(1, yb)).astype(BF16)
        d = remote(swap_out.at[t], swap_in.at[t], sw_s.at[t], sw_r.at[t], other)
        d.start()
        swaps.append(d)
    for t in range(Y // 2):
        yb = c * (Y // 2) + t
        mine_t = acc[yb].reshape(R, acc.shape[-1]) + product(1, yb)
        swaps[t].wait_recv()
        den_ref[pl.ds(t * R, R), :] = (mine_t + swap_in[t].astype(F32)).astype(BF16)
    for chunk in range(chunks):
        left(got1.at[pl.ds(2 * chunk, 2)], n3_s.at[chunk], n3_r.at[chunk])
    for d in sent + swaps:
        d.wait_send()


def local(dims, mul, integ, amp, slab, slab_amp, rest, occupied, virtual):
    Y, X, Z = dims
    N = Y
    B = 8 * Z
    R = Y * X * B
    C = CHUNKS
    S = 2 * C
    p, q = mul.shape
    W = p // S
    dma = pltpu.SemaphoreType.DMA
    vmem = pl.BlockSpec(memory_space=pltpu.VMEM)
    hbm = pl.BlockSpec(memory_space=pltpu.HBM)
    scratch = [
        pltpu.VMEM((p, q), BF16),
        pltpu.VMEM((q, R), BF16),
        pltpu.VMEM((p, q), BF16),
        pltpu.VMEM((8, p), BF16),
        pltpu.VMEM((8, p), BF16),
        pltpu.VMEM((p,), BF16),
        pltpu.VMEM((8,), BF16),
        pltpu.VMEM((S, Y, X, B, W), BF16),
        pltpu.VMEM((S, N - 1, N, B, W), BF16),
        pltpu.VMEM((S, N - 1, B, W), BF16),
        pltpu.VMEM((S, N - 1, B, W), BF16),
        pltpu.VMEM((C, B, 2 * W), F32),
        pltpu.VMEM((C, Z, 8, 2 * W), BF16),
        pltpu.VMEM((C, Z - 1, 8, 2 * W), BF16),
        pltpu.VMEM((C, Z, 8, 2 * W), BF16),
        pltpu.VMEM((Y, X, B, p), BF16),
        pltpu.VMEM((Z, Y, X, 8, p), BF16),
        pltpu.VMEM((Y, X, Z, 8, q), F32),
        pltpu.VMEM((Y // 2, R // Y, q), BF16),
        pltpu.VMEM((Y // 2, R // Y, q), BF16),
        dma((8,)),
        *[dma((C,)) for _ in range(12)],
        dma((X - 1,)), dma((X - 1,)),
        dma((Y - 1,)), dma((Y - 1,)),
        dma((2, Z // 2)), dma((2, Z // 2)),
        dma((Y // 2,)), dma((Y // 2,)),
    ]
    return pl.pallas_call(
        functools.partial(kernel, dims),
        out_shape=(
            jax.ShapeDtypeStruct((8, p), BF16),
            jax.ShapeDtypeStruct((R // 2, q), BF16),
        ),
        in_specs=[hbm] * 8,
        out_specs=(vmem, vmem),
        scratch_shapes=scratch,
        compiler_params=pltpu.CompilerParams(
            collective_id=0, has_side_effects=True, vmem_limit_bytes=50 * 1024 * 1024
        ),
        name="ladder_step",
    )(*[pltpu.with_memory_space_constraint(a, pltpu.HBM) for a in (mul, integ, amp, slab, slab_amp, rest, occupied, virtual)])


def solution(mesh, dims=(4, 4, 8)):
    placed = (
        P("op", "vp"),
        P("vp", None),
        P("op", "vp"),
        P("vp", "op"),
        P("vp", "op"),
        P("vp", "op"),
        P("op"),
        P("vp"),
    )
    return jax.shard_map(
        functools.partial(local, dims), mesh=mesh, in_specs=placed,
        out_specs=(P("vp", "op"), P("op", "vp")), check_vma=False,
    )
```

```python
import functools

import jax
import jax.numpy as jnp
from jax import lax
from jax.experimental import pallas as pl
from jax.experimental.pallas import tpu as pltpu
from jax.sharding import PartitionSpec as P

F32 = jnp.float32
BF16 = jnp.bfloat16
CHUNKS = 4


def kernel(
    dims,
    mul_hbm, int_hbm, amp_hbm, slab_hbm, slab_amp_hbm, rest_hbm, occ_hbm, virt_hbm,
    new_ref, den_ref,
    mul, integ, amp, slab, rest, occ, virt,
    lad, got1, sum1, got2, own3, sum2, got3, new_z, new_all, am_all, am_z, am_full, acc,
    swap_out, swap_in,
    load_sem, s1, r1, s2, r2, s3, r3, nz_s, nz_r, n2_s, n2_r, n3_s, n3_r,
    ax_s, ax_r, ay_s, ay_r, az_s, az_r, ag_s, ag_r, sw_s, sw_r,
):
    Y, X, Z = dims
    N = Y
    v = lax.axis_index("vp")
    c = lax.axis_index("op")
    y = v // (X * Z)
    x = lax.rem(v // Z, X)
    z = lax.rem(v, Z)
    B = 8 * Z
    R = X * B
    W = lad.shape[-1]
    chunks = lad.shape[0] // 2
    A = am_z.shape[-1]
    V = A // 2

    def near(axis, k):
        return lax.rem((y, x, z)[axis] + k, dims[axis])

    def at(axis, i):
        if axis == 0:
            return {"vp": (i * X + x) * Z + z}
        if axis == 1:
            return {"vp": (y * X + i) * Z + z}
        return {"vp": (y * X + x) * Z + i}

    other = {"op": 1 - c}
    sent = []

    def remote(src, dst, ss, rs, device):
        return pltpu.make_async_remote_copy(
            src_ref=src, dst_ref=dst, send_sem=ss, recv_sem=rs,
            device_id=device, device_id_type=pl.DeviceIdType.MESH,
        )

    def send(src, dst, ss, rs, device):
        d = remote(src, dst, ss, rs, device)
        d.start()
        sent.append(d)

    def arrived(ref, ss, rs, device):
        remote(ref, ref, ss, rs, device).wait_recv()

    def post(src, dst, ss, rs, device):
        remote(src, dst, ss, rs, device).start()

    def landed(bulk, ss, rs):
        remote(bulk, bulk, ss, rs, other).wait_recv()

    def left(bulk, ss, rs):
        remote(bulk, bulk, ss, rs, other).wait_send()

    loads = [
        pltpu.make_async_copy(src, dst, load_sem.at[i])
        for i, (src, dst) in enumerate([
            (slab_amp_hbm.at[:, pl.ds(A, mul.shape[0] - A)], am_all.at[z, y, x]),
            (int_hbm, integ), (mul_hbm, mul),
            (slab_amp_hbm.at[:, pl.ds(0, A)], am_z.at[z]),
            (slab_hbm, slab), (rest_hbm, rest), (occ_hbm, occ), (virt_hbm, virt), (amp_hbm, amp),
        ])
    ]
    for d in loads:
        d.start()

    barrier = pltpu.get_barrier_semaphore()
    greet = [at(a, near(a, k)) for a in range(3) for k in range(1, dims[a])] + [other]
    for device in greet:
        pl.semaphore_signal(barrier, inc=1, device_id=device, device_id_type=pl.DeviceIdType.MESH)
    def amp_own():
        mine = am_all.at[z, y, x]
        for k in range(1, X):
            send(mine, mine, ax_s.at[k - 1], ax_r.at[X - 1 - k], at(1, near(1, k)))

    def amp_rows():
        for i in range(X - 1):
            arrived(am_all.at[z, y, near(1, i + 1)], ax_s.at[i], ax_r.at[i], at(1, near(1, i + 1)))
        row = am_all.at[z, y]
        for k in range(1, Y):
            send(row, row, ay_s.at[k - 1], ay_r.at[Y - 1 - k], at(0, near(0, k)))

    H = Z // 2

    def ring_piece(side, step):
        block = near(2, Z - (step - 1)) if side == 0 else near(2, step - 1)
        if step < H:
            return am_all.at[block]
        return am_all.at[block, pl.ds(side * (Y // 2), Y // 2)]

    def ring_landed(side, step):
        block = near(2, Z - step) if side == 0 else near(2, step)
        if step < H:
            return am_all.at[block]
        return am_all.at[block, pl.ds(side * (Y // 2), Y // 2)]

    def ring_wait(step):
        for side in range(2):
            arrived(
                ring_landed(side, step), az_s.at[side, step - 1], az_r.at[side, step - 1],
                at(2, near(2, 1 if side == 0 else Z - 1)),
            )

    def ring_step(step):
        if step == 1:
            for i in range(Y - 1):
                arrived(am_all.at[z, near(0, i + 1)], ay_s.at[i], ay_r.at[i], at(0, near(0, i + 1)))
        else:
            ring_wait(step - 1)
        for side in range(2):
            piece = ring_piece(side, step)
            send(
                piece, piece, az_s.at[side, step - 1], az_r.at[side, step - 1],
                at(2, near(2, 1 if side == 0 else Z - 1)),
            )

    def axes(s):
        return (1, 0) if s % 2 == 0 else (0, 1)

    def ladder(part):
        streams = range(part * chunks, (part + 1) * chunks)
        lo = part * chunks * W
        for n in range(N):
            tile = lax.dot_general(
                integ[:, n * R:(n + 1) * R], mul[lo:lo + chunks * W, :],
                (((0,), (1,)), ((), ())), preferred_element_type=F32,
            )
            for s in streams:
                piece = tile[:, s * W - lo:(s + 1) * W - lo].astype(BF16).reshape(X, B, W)
                if s % 2 == 0:
                    lad[s, :, n] = piece
                else:
                    lad[s, n] = piece

    def ladder_send(chunk):
        for k in (2, 1, 3) if N == 4 else range(1, N):
            for s in (2 * chunk, 2 * chunk + 1):
                one = axes(s)[0]
                j = near(one, k)
                post(lad.at[s, j], got1.at[s, N - 1 - k], s1.at[chunk], r1.at[chunk], at(one, j))

    def ladder_next(chunk):
        left(got1.at[pl.ds(2 * chunk, 2)], s1.at[chunk], r1.at[chunk])
        ladder_send(chunk + 1)

    def sum_first(chunk):
        landed(got1.at[pl.ds(2 * chunk, 2)], s1.at[chunk], r1.at[chunk])
        for s in (2 * chunk + 1, 2 * chunk):
            one, two = axes(s)
            me = (y, x)[one]
            for n in range(N):
                k = n + 1
                b = near(two, k)
                total = lad[s, me, b].astype(F32)
                for i in range(N - 1):
                    total = total + got1[s, i, b].astype(F32)
                if k < N:
                    sum1[s, n] = total.astype(BF16)
                    post(
                        sum1.at[s, n], got2.at[s, N - 1 - k], s2.at[chunk], r2.at[chunk], at(two, b)
                    )
                else:
                    own3[chunk, :, (s % 2) * W:(s % 2 + 1) * W] = total

    def sum_second(chunk):
        landed(got2.at[pl.ds(2 * chunk, 2)], s2.at[chunk], r2.at[chunk])
        for o in range(2):
            s = 2 * chunk + o
            two = axes(s)[1]
            cols = slice(o * W, (o + 1) * W)
            total = own3[chunk, :, cols]
            for i in range(N - 1):
                total = total + got2[s, i].astype(F32)
            own3[chunk, :, cols] = total
            sum2[chunk, :, :, cols] = total.reshape(Z, 8, W).astype(BF16)
        for k in range(1, Z):
            zb = near(2, k)
            post(
                sum2.at[chunk, zb], got3.at[chunk, Z - 1 - k], s3.at[chunk], r3.at[chunk], at(2, zb)
            )

    def renew(chunk):
        cols = slice(chunk * 2 * W, (chunk + 1) * 2 * W)
        landed(got3.at[chunk], s3.at[chunk], r3.at[chunk])
        total = own3[chunk, pl.ds(pl.multiple_of(z * 8, 8), 8), :]
        for i in range(Z - 1):
            total = total + got3[chunk, i].astype(F32)
        row = lax.broadcasted_iota(jnp.int32, (8, 8), 0)
        col = lax.broadcasted_iota(jnp.int32, (8, 8), 1)
        energy = jnp.broadcast_to(virt[...].astype(F32).reshape(1, 8), (8, 8))
        energy = jnp.sum(jnp.where(row == col, energy, 0.0), axis=1, keepdims=True)
        divisor = energy - occ[cols].astype(F32).reshape(1, 2 * W)
        renewed = slab[:, cols].astype(F32) + (total + rest[:, cols].astype(F32)) / divisor
        renewed = renewed.astype(BF16)
        new_ref[:, cols] = renewed
        new_z[chunk, z] = renewed
        here = new_z.at[chunk, z]
        for k in range(1, Z):
            post(here, here, nz_s.at[chunk], nz_r.at[chunk], at(2, near(2, k)))

    def spread_own(chunk):
        landed(got3.at[chunk], nz_s.at[chunk], nz_r.at[chunk])
        whole = new_z[chunk].astype(F32).reshape(B, 2 * W).astype(BF16)
        new_all[y, x, :, chunk * 2 * W:(chunk + 1) * 2 * W] = whole
        for k in (2, 1, 3) if N == 4 else range(1, N):
            for s in (2 * chunk, 2 * chunk + 1):
                two = axes(s)[1]
                here = new_all.at[y, x, :, pl.ds(s * W, W)]
                post(here, here, n2_s.at[chunk], n2_r.at[chunk], at(two, near(two, k)))

    def spread_got(chunk):
        landed(got2.at[pl.ds(2 * chunk, 2)], n2_s.at[chunk], n2_r.at[chunk])
        for k in (2, 1, 3) if N == 4 else range(1, N):
            for s in (2 * chunk, 2 * chunk + 1):
                one = axes(s)[0]
                cols = pl.ds(s * W, W)
                here = new_all.at[:, x, :, cols] if s % 2 == 0 else new_all.at[y, :, :, cols]
                post(here, here, n3_s.at[chunk], n3_r.at[chunk], at(one, near(one, k)))

    def spread_wait(chunk):
        landed(got1.at[pl.ds(2 * chunk, 2)], n3_s.at[chunk], n3_r.at[chunk])

    def all_left(chunk):
        pair = pl.ds(2 * chunk, 2)
        if chunk == chunks - 1:
            left(got1.at[pair], s1.at[chunk], r1.at[chunk])
        left(got2.at[pair], s2.at[chunk], r2.at[chunk])
        left(got3.at[chunk], s3.at[chunk], r3.at[chunk])
        left(got3.at[chunk], nz_s.at[chunk], nz_r.at[chunk])
        left(got2.at[pair], n2_s.at[chunk], n2_r.at[chunk])

    def staged_z():
        here = am_z.at[z]
        for k in range(1, Z):
            post(here, here, ag_s.at[0], ag_r.at[0], at(2, near(2, k)))

    def staged_own():
        landed(am_z.at[pl.ds(0, Z - 1)], ag_s.at[0], ag_r.at[0])
        am_full[y, x] = am_z[...].astype(F32).reshape(B, A).astype(BF16)
        for k in range(1, N):
            for o in range(2):
                here = am_full.at[y, x, :, pl.ds(o * V, V)]
                post(here, here, ag_s.at[1], ag_r.at[1], at(axes(o)[1], near(axes(o)[1], k)))

    def staged_got():
        landed(am_full.at[0, pl.ds(0, N - 1)], ag_s.at[1], ag_r.at[1])
        for k in range(1, N):
            for o in range(2):
                cols = pl.ds(o * V, V)
                here = am_full.at[:, x, :, cols] if o == 0 else am_full.at[y, :, :, cols]
                post(here, here, ag_s.at[2], ag_r.at[2], at(axes(o)[0], near(axes(o)[0], k)))

    def staged_wait():
        landed(am_full.at[pl.ds(0, N - 1)], ag_s.at[2], ag_r.at[2])
        left(am_z.at[pl.ds(0, Z - 1)], ag_s.at[0], ag_r.at[0])
        left(am_full.at[0, pl.ds(0, N - 1)], ag_s.at[1], ag_r.at[1])
        left(am_full.at[pl.ds(0, N - 1)], ag_s.at[2], ag_r.at[2])

    def amp_part(zb):
        rows = am_all[zb].astype(F32).reshape(Y * X * 8, mul.shape[0] - A).astype(BF16)
        acc[:, :, zb] = jnp.dot(rows, mul[A:, :], preferred_element_type=F32).reshape(Y, X, 8, acc.shape[-1])

    K = mul.shape[0] // 2

    def product(half, yb):
        left = new_all[yb, :, :, half * K:(half + 1) * K].reshape(R, K)
        return jnp.dot(left, amp[half * K:(half + 1) * K, :], preferred_element_type=F32)

    loads[1].wait()
    loads[2].wait()
    ladder(0)
    loads[0].wait()
    loads[3].wait()
    pl.semaphore_wait(barrier, len(greet))
    amp_own()
    staged_z()
    ladder_send(0)
    ladder(1)
    ladder_next(0)
    amp_rows()
    for d in loads[4:]:
        d.wait()
    sum_first(0)
    ladder_next(1)
    staged_own()
    sum_first(1)
    ladder_next(2)
    ring_step(1)
    sum_second(0)
    sum_first(2)
    sum_second(1)
    sum_first(3)
    staged_got()
    amp_part(z)
    renew(0)
    sum_second(2)
    ring_step(2)
    renew(1)
    sum_second(3)
    amp_part(near(2, 1))
    amp_part(near(2, Z - 1))
    spread_own(0)
    renew(2)
    ring_step(3)
    spread_own(1)
    renew(3)
    spread_got(0)
    amp_part(near(2, 2))
    amp_part(near(2, Z - 2))
    spread_own(2)
    spread_got(1)
    ring_step(4)
    spread_own(3)
    spread_got(2)
    amp_part(near(2, 3))
    amp_part(near(2, Z - 3))
    spread_got(3)
    ring_wait(4)
    amp_part(near(2, H))
    staged_wait()
    for chunk in range(chunks):
        all_left(chunk)
    for chunk in range(chunks // 2):
        spread_wait(chunk)

    @pl.loop(0, Y)
    def _(t):
        staged = jnp.dot(am_full[t].reshape(R, A), mul[:A, :], preferred_element_type=F32)
        acc[t] = acc[t] + (product(0, t) + staged).reshape(acc.shape[1:])

    for chunk in range(chunks // 2, chunks):
        spread_wait(chunk)
    swaps = []
    for t in range(Y // 2):
        yb = (1 - c) * (Y // 2) + t
        swap_out[t] = (acc[yb].reshape(R, acc.shape[-1]) + product(1, yb)).astype(BF16)
        d = remote(swap_out.at[t], swap_in.at[t], sw_s.at[t], sw_r.at[t], other)
        d.start()
        swaps.append(d)
    for t in range(Y // 2):
        yb = c * (Y // 2) + t
        mine_t = acc[yb].reshape(R, acc.shape[-1]) + product(1, yb)
        swaps[t].wait_recv()
        den_ref[pl.ds(t * R, R), :] = (mine_t + swap_in[t].astype(F32)).astype(BF16)
    for chunk in range(chunks):
        left(got1.at[pl.ds(2 * chunk, 2)], n3_s.at[chunk], n3_r.at[chunk])
    for d in sent + swaps:
        d.wait_send()


def local(dims, mul, integ, amp, slab, slab_amp, rest, occupied, virtual):
    Y, X, Z = dims
    N = Y
    B = 8 * Z
    R = Y * X * B
    C = CHUNKS
    S = 2 * C
    p, q = mul.shape
    W = p // S
    A = p // 2
    dma = pltpu.SemaphoreType.DMA
    vmem = pl.BlockSpec(memory_space=pltpu.VMEM)
    hbm = pl.BlockSpec(memory_space=pltpu.HBM)
    scratch = [
        pltpu.VMEM((p, q), BF16),
        pltpu.VMEM((q, R), BF16),
        pltpu.VMEM((p, q), BF16),
        pltpu.VMEM((8, p), BF16),
        pltpu.VMEM((8, p), BF16),
        pltpu.VMEM((p,), BF16),
        pltpu.VMEM((8,), BF16),
        pltpu.VMEM((S, Y, X, B, W), BF16),
        pltpu.VMEM((S, N - 1, N, B, W), BF16),
        pltpu.VMEM((S, N - 1, B, W), BF16),
        pltpu.VMEM((S, N - 1, B, W), BF16),
        pltpu.VMEM((C, B, 2 * W), F32),
        pltpu.VMEM((C, Z, 8, 2 * W), BF16),
        pltpu.VMEM((C, Z - 1, 8, 2 * W), BF16),
        pltpu.VMEM((C, Z, 8, 2 * W), BF16),
        pltpu.VMEM((Y, X, B, p), BF16),
        pltpu.VMEM((Z, Y, X, 8, p - A), BF16),
        pltpu.VMEM((Z, 8, A), BF16),
        pltpu.VMEM((Y, X, B, A), BF16),
        pltpu.VMEM((Y, X, Z, 8, q), F32),
        pltpu.VMEM((Y // 2, R // Y, q), BF16),
        pltpu.VMEM((Y // 2, R // Y, q), BF16),
        dma((9,)),
        *[dma((C,)) for _ in range(12)],
        dma((X - 1,)), dma((X - 1,)),
        dma((Y - 1,)), dma((Y - 1,)),
        dma((2, Z // 2)), dma((2, Z // 2)),
        dma((3,)), dma((3,)),
        dma((Y // 2,)), dma((Y // 2,)),
    ]
    return pl.pallas_call(
        functools.partial(kernel, dims),
        out_shape=(
            jax.ShapeDtypeStruct((8, p), BF16),
            jax.ShapeDtypeStruct((R // 2, q), BF16),
        ),
        in_specs=[hbm] * 8,
        out_specs=(vmem, vmem),
        scratch_shapes=scratch,
        compiler_params=pltpu.CompilerParams(
            collective_id=0, has_side_effects=True, vmem_limit_bytes=50 * 1024 * 1024
        ),
        name="ladder_step",
    )(*[pltpu.with_memory_space_constraint(a, pltpu.HBM) for a in (mul, integ, amp, slab, slab_amp, rest, occupied, virtual)])


def solution(mesh, dims=(4, 4, 8)):
    placed = (
        P("op", "vp"),
        P("vp", None),
        P("op", "vp"),
        P("vp", "op"),
        P("vp", "op"),
        P("vp", "op"),
        P("op"),
        P("vp"),
    )
    return jax.shard_map(
        functools.partial(local, dims), mesh=mesh, in_specs=placed,
        out_specs=(P("vp", "op"), P("op", "vp")), check_vma=False,
    )
```

```python
import functools

import jax
import jax.numpy as jnp
from jax import lax
from jax.experimental import pallas as pl
from jax.experimental.pallas import tpu as pltpu
from jax.sharding import PartitionSpec as P

F32 = jnp.float32
BF16 = jnp.bfloat16
CHUNKS = 4


def kernel(
    dims,
    mul_hbm, int_hbm, amp_hbm, slab_hbm, slab_amp_hbm, rest_hbm, occ_hbm, virt_hbm,
    new_ref, den_ref,
    mul, integ, amp, slab, rest, occ, virt,
    lad, got1, sum1, got2, own3, sum2, got3, new_z, new_all, am_all, am_z, am_full, acc,
    swap_out, swap_in,
    load_sem, s1, r1, s2, r2, s3, r3, nz_s, nz_r, n2_s, n2_r, n3_s, n3_r,
    ax_s, ax_r, ay_s, ay_r, az_s, az_r, ag_s, ag_r, sw_s, sw_r,
):
    Y, X, Z = dims
    N = Y
    v = lax.axis_index("vp")
    c = lax.axis_index("op")
    y = v // (X * Z)
    x = lax.rem(v // Z, X)
    z = lax.rem(v, Z)
    B = 8 * Z
    R = X * B
    W = lad.shape[-1]
    chunks = lad.shape[0] // 2
    A = am_z.shape[-1]
    V = A // 2

    def near(axis, k):
        return lax.rem((y, x, z)[axis] + k, dims[axis])

    def at(axis, i):
        if axis == 0:
            return {"vp": (i * X + x) * Z + z}
        if axis == 1:
            return {"vp": (y * X + i) * Z + z}
        return {"vp": (y * X + x) * Z + i}

    other = {"op": 1 - c}

    def far_first(n):
        return sorted(range(1, n), key=lambda k: -min(k, n - k))

    sent = []

    def remote(src, dst, ss, rs, device):
        return pltpu.make_async_remote_copy(
            src_ref=src, dst_ref=dst, send_sem=ss, recv_sem=rs,
            device_id=device, device_id_type=pl.DeviceIdType.MESH,
        )

    def send(src, dst, ss, rs, device):
        d = remote(src, dst, ss, rs, device)
        d.start()
        sent.append(d)

    def arrived(ref, ss, rs, device):
        remote(ref, ref, ss, rs, device).wait_recv()

    def post(src, dst, ss, rs, device):
        remote(src, dst, ss, rs, device).start()

    def landed(bulk, ss, rs):
        remote(bulk, bulk, ss, rs, other).wait_recv()

    def left(bulk, ss, rs):
        remote(bulk, bulk, ss, rs, other).wait_send()

    loads = [
        pltpu.make_async_copy(src, dst, load_sem.at[i])
        for i, (src, dst) in enumerate([
            (slab_amp_hbm.at[:, pl.ds(A, mul.shape[0] - A)], am_all.at[z, y, x]),
            (int_hbm, integ), (mul_hbm, mul),
            (slab_amp_hbm.at[:, pl.ds(0, A)], am_z.at[z]),
            (slab_hbm, slab), (rest_hbm, rest), (occ_hbm, occ), (virt_hbm, virt), (amp_hbm, amp),
        ])
    ]
    for d in loads:
        d.start()

    barrier = pltpu.get_barrier_semaphore()
    greet = [at(a, near(a, k)) for a in range(3) for k in range(1, dims[a])] + [other]
    for device in greet:
        pl.semaphore_signal(barrier, inc=1, device_id=device, device_id_type=pl.DeviceIdType.MESH)
    def amp_own():
        mine = am_all.at[z, y, x]
        for k in range(1, X):
            send(mine, mine, ax_s.at[k - 1], ax_r.at[X - 1 - k], at(1, near(1, k)))

    def amp_rows():
        for i in range(X - 1):
            arrived(am_all.at[z, y, near(1, i + 1)], ax_s.at[i], ax_r.at[i], at(1, near(1, i + 1)))
        row = am_all.at[z, y]
        for k in range(1, Y):
            send(row, row, ay_s.at[k - 1], ay_r.at[Y - 1 - k], at(0, near(0, k)))

    H = Z // 2

    def ring_piece(side, step):
        block = near(2, Z - (step - 1)) if side == 0 else near(2, step - 1)
        if step < H:
            return am_all.at[block]
        return am_all.at[block, pl.ds(side * (Y // 2), Y // 2)]

    def ring_landed(side, step):
        block = near(2, Z - step) if side == 0 else near(2, step)
        if step < H:
            return am_all.at[block]
        return am_all.at[block, pl.ds(side * (Y // 2), Y // 2)]

    def ring_wait(step):
        for side in range(2):
            arrived(
                ring_landed(side, step), az_s.at[side, step - 1], az_r.at[side, step - 1],
                at(2, near(2, 1 if side == 0 else Z - 1)),
            )

    def ring_step(step):
        if step == 1:
            for i in range(Y - 1):
                arrived(am_all.at[z, near(0, i + 1)], ay_s.at[i], ay_r.at[i], at(0, near(0, i + 1)))
        else:
            ring_wait(step - 1)
        for side in range(2):
            piece = ring_piece(side, step)
            send(
                piece, piece, az_s.at[side, step - 1], az_r.at[side, step - 1],
                at(2, near(2, 1 if side == 0 else Z - 1)),
            )

    def axes(s):
        return (1, 0) if s % 2 == 0 else (0, 1)

    def ladder(part):
        streams = range(part * chunks, (part + 1) * chunks)
        lo = part * chunks * W
        for n in range(N):
            tile = lax.dot_general(
                integ[:, n * R:(n + 1) * R], mul[lo:lo + chunks * W, :],
                (((0,), (1,)), ((), ())), preferred_element_type=F32,
            )
            for s in streams:
                piece = tile[:, s * W - lo:(s + 1) * W - lo].astype(BF16).reshape(X, B, W)
                if s % 2 == 0:
                    lad[s, :, n] = piece
                else:
                    lad[s, n] = piece

    def ladder_send(chunk):
        for k in far_first(N):
            for s in (2 * chunk, 2 * chunk + 1):
                one = axes(s)[0]
                j = near(one, k)
                post(lad.at[s, j], got1.at[s, N - 1 - k], s1.at[chunk], r1.at[chunk], at(one, j))

    def ladder_next(chunk):
        left(got1.at[pl.ds(2 * chunk, 2)], s1.at[chunk], r1.at[chunk])
        ladder_send(chunk + 1)

    def sum_first(chunk):
        landed(got1.at[pl.ds(2 * chunk, 2)], s1.at[chunk], r1.at[chunk])
        for s in (2 * chunk + 1, 2 * chunk):
            one, two = axes(s)
            me = (y, x)[one]
            for k in far_first(N) + [N]:
                n = k - 1
                b = near(two, k)
                total = lad[s, me, b].astype(F32)
                for i in range(N - 1):
                    total = total + got1[s, i, b].astype(F32)
                if k < N:
                    sum1[s, n] = total.astype(BF16)
                    post(
                        sum1.at[s, n], got2.at[s, N - 1 - k], s2.at[chunk], r2.at[chunk], at(two, b)
                    )
                else:
                    own3[chunk, :, (s % 2) * W:(s % 2 + 1) * W] = total

    def sum_second(chunk):
        landed(got2.at[pl.ds(2 * chunk, 2)], s2.at[chunk], r2.at[chunk])
        for o in range(2):
            s = 2 * chunk + o
            two = axes(s)[1]
            cols = slice(o * W, (o + 1) * W)
            total = own3[chunk, :, cols]
            for i in range(N - 1):
                total = total + got2[s, i].astype(F32)
            own3[chunk, :, cols] = total
            sum2[chunk, :, :, cols] = total.reshape(Z, 8, W).astype(BF16)
        for k in far_first(Z):
            zb = near(2, k)
            post(
                sum2.at[chunk, zb], got3.at[chunk, Z - 1 - k], s3.at[chunk], r3.at[chunk], at(2, zb)
            )

    def renew(chunk):
        cols = slice(chunk * 2 * W, (chunk + 1) * 2 * W)
        landed(got3.at[chunk], s3.at[chunk], r3.at[chunk])
        total = own3[chunk, pl.ds(pl.multiple_of(z * 8, 8), 8), :]
        for i in range(Z - 1):
            total = total + got3[chunk, i].astype(F32)
        row = lax.broadcasted_iota(jnp.int32, (8, 8), 0)
        col = lax.broadcasted_iota(jnp.int32, (8, 8), 1)
        energy = jnp.broadcast_to(virt[...].astype(F32).reshape(1, 8), (8, 8))
        energy = jnp.sum(jnp.where(row == col, energy, 0.0), axis=1, keepdims=True)
        divisor = energy - occ[cols].astype(F32).reshape(1, 2 * W)
        renewed = slab[:, cols].astype(F32) + (total + rest[:, cols].astype(F32)) / divisor
        renewed = renewed.astype(BF16)
        new_ref[:, cols] = renewed
        new_z[chunk, z] = renewed
        here = new_z.at[chunk, z]
        for k in far_first(Z):
            post(here, here, nz_s.at[chunk], nz_r.at[chunk], at(2, near(2, k)))

    def spread_own(chunk):
        landed(got3.at[chunk], nz_s.at[chunk], nz_r.at[chunk])
        whole = new_z[chunk].astype(F32).reshape(B, 2 * W).astype(BF16)
        new_all[y, x, :, chunk * 2 * W:(chunk + 1) * 2 * W] = whole
        for k in far_first(N):
            for s in (2 * chunk, 2 * chunk + 1):
                two = axes(s)[1]
                here = new_all.at[y, x, :, pl.ds(s * W, W)]
                post(here, here, n2_s.at[chunk], n2_r.at[chunk], at(two, near(two, k)))
        for k in far_first(N):
            for s in (2 * chunk, 2 * chunk + 1):
                one = axes(s)[0]
                here = new_all.at[y, x, :, pl.ds(s * W, W)]
                post(here, here, n3_s.at[chunk], n3_r.at[chunk], at(one, near(one, k)))

    def spread_got(chunk):
        landed(got2.at[pl.ds(2 * chunk, 2)], n2_s.at[chunk], n2_r.at[chunk])
        for k in far_first(N):
            for i in far_first(N):
                for s in (2 * chunk, 2 * chunk + 1):
                    one, two = axes(s)
                    cols = pl.ds(s * W, W)
                    b = near(two, i)
                    here = new_all.at[b, x, :, cols] if s % 2 == 0 else new_all.at[y, b, :, cols]
                    post(here, here, n3_s.at[chunk], n3_r.at[chunk], at(one, near(one, k)))

    def spread_wait(chunk):
        landed(got1.at[pl.ds(2 * chunk, 2)], n3_s.at[chunk], n3_r.at[chunk])

    def all_left(chunk):
        pair = pl.ds(2 * chunk, 2)
        if chunk == chunks - 1:
            left(got1.at[pair], s1.at[chunk], r1.at[chunk])
        left(got2.at[pair], s2.at[chunk], r2.at[chunk])
        left(got3.at[chunk], s3.at[chunk], r3.at[chunk])
        left(got3.at[chunk], nz_s.at[chunk], nz_r.at[chunk])
        left(got2.at[pair], n2_s.at[chunk], n2_r.at[chunk])

    def staged_z():
        here = am_z.at[z]
        for k in far_first(Z):
            post(here, here, ag_s.at[0], ag_r.at[0], at(2, near(2, k)))

    def staged_own():
        landed(am_z.at[pl.ds(0, Z - 1)], ag_s.at[0], ag_r.at[0])
        am_full[y, x] = am_z[...].astype(F32).reshape(B, A).astype(BF16)
        for k in range(1, N):
            for o in range(2):
                here = am_full.at[y, x, :, pl.ds(o * V, V)]
                post(here, here, ag_s.at[1], ag_r.at[1], at(axes(o)[1], near(axes(o)[1], k)))

    def staged_got():
        landed(am_full.at[0, pl.ds(0, N - 1)], ag_s.at[1], ag_r.at[1])
        for k in range(1, N):
            for o in range(2):
                cols = pl.ds(o * V, V)
                here = am_full.at[:, x, :, cols] if o == 0 else am_full.at[y, :, :, cols]
                post(here, here, ag_s.at[2], ag_r.at[2], at(axes(o)[0], near(axes(o)[0], k)))

    def staged_wait():
        landed(am_full.at[pl.ds(0, N - 1)], ag_s.at[2], ag_r.at[2])
        left(am_z.at[pl.ds(0, Z - 1)], ag_s.at[0], ag_r.at[0])
        left(am_full.at[0, pl.ds(0, N - 1)], ag_s.at[1], ag_r.at[1])
        left(am_full.at[pl.ds(0, N - 1)], ag_s.at[2], ag_r.at[2])

    def amp_part(zb):
        rows = am_all[zb].astype(F32).reshape(Y * X * 8, mul.shape[0] - A).astype(BF16)
        acc[:, :, zb] = jnp.dot(rows, mul[A:, :], preferred_element_type=F32).reshape(Y, X, 8, acc.shape[-1])

    K = mul.shape[0] // 2

    def product(half, yb):
        left = new_all[yb, :, :, half * K:(half + 1) * K].reshape(R, K)
        return jnp.dot(left, amp[half * K:(half + 1) * K, :], preferred_element_type=F32)

    loads[1].wait()
    loads[2].wait()
    ladder(0)
    loads[0].wait()
    loads[3].wait()
    pl.semaphore_wait(barrier, len(greet))
    amp_own()
    staged_z()
    ladder_send(0)
    ladder(1)
    ladder_next(0)
    amp_rows()
    for d in loads[4:]:
        d.wait()
    sum_first(0)
    ladder_next(1)
    sum_first(1)
    ladder_next(2)
    staged_own()
    ring_step(1)
    sum_second(0)
    sum_first(2)
    sum_second(1)
    sum_first(3)
    renew(0)
    sum_second(2)
    staged_got()
    ring_step(2)
    renew(1)
    sum_second(3)
    spread_own(0)
    renew(2)
    ring_step(3)
    spread_own(1)
    renew(3)
    spread_got(0)
    spread_own(2)
    spread_got(1)
    ring_step(4)
    spread_own(3)
    spread_got(2)
    spread_got(3)
    amp_part(z)
    for k in range(1, H):
        amp_part(near(2, k))
        amp_part(near(2, Z - k))
    ring_wait(4)
    amp_part(near(2, H))
    staged_wait()
    for chunk in range(chunks):
        all_left(chunk)
    for chunk in range(chunks // 2):
        spread_wait(chunk)

    @pl.loop(0, Y)
    def _(t):
        staged = jnp.dot(am_full[t].reshape(R, A), mul[:A, :], preferred_element_type=F32)
        acc[t] = acc[t] + (product(0, t) + staged).reshape(acc.shape[1:])

    for chunk in range(chunks // 2, chunks):
        spread_wait(chunk)
    swaps = []
    for t in range(Y // 2):
        yb = (1 - c) * (Y // 2) + t
        swap_out[t] = (acc[yb].reshape(R, acc.shape[-1]) + product(1, yb)).astype(BF16)
        d = remote(swap_out.at[t], swap_in.at[t], sw_s.at[t], sw_r.at[t], other)
        d.start()
        swaps.append(d)
    for t in range(Y // 2):
        yb = c * (Y // 2) + t
        mine_t = acc[yb].reshape(R, acc.shape[-1]) + product(1, yb)
        swaps[t].wait_recv()
        den_ref[pl.ds(t * R, R), :] = (mine_t + swap_in[t].astype(F32)).astype(BF16)
    for chunk in range(chunks):
        left(got1.at[pl.ds(2 * chunk, 2)], n3_s.at[chunk], n3_r.at[chunk])
    for d in sent + swaps:
        d.wait_send()


def local(dims, mul, integ, amp, slab, slab_amp, rest, occupied, virtual):
    Y, X, Z = dims
    N = Y
    B = 8 * Z
    R = Y * X * B
    C = CHUNKS
    S = 2 * C
    p, q = mul.shape
    W = p // S
    A = p // 2
    dma = pltpu.SemaphoreType.DMA
    vmem = pl.BlockSpec(memory_space=pltpu.VMEM)
    hbm = pl.BlockSpec(memory_space=pltpu.HBM)
    scratch = [
        pltpu.VMEM((p, q), BF16),
        pltpu.VMEM((q, R), BF16),
        pltpu.VMEM((p, q), BF16),
        pltpu.VMEM((8, p), BF16),
        pltpu.VMEM((8, p), BF16),
        pltpu.VMEM((p,), BF16),
        pltpu.VMEM((8,), BF16),
        pltpu.VMEM((S, Y, X, B, W), BF16),
        pltpu.VMEM((S, N - 1, N, B, W), BF16),
        pltpu.VMEM((S, N - 1, B, W), BF16),
        pltpu.VMEM((S, N - 1, B, W), BF16),
        pltpu.VMEM((C, B, 2 * W), F32),
        pltpu.VMEM((C, Z, 8, 2 * W), BF16),
        pltpu.VMEM((C, Z - 1, 8, 2 * W), BF16),
        pltpu.VMEM((C, Z, 8, 2 * W), BF16),
        pltpu.VMEM((Y, X, B, p), BF16),
        pltpu.VMEM((Z, Y, X, 8, p - A), BF16),
        pltpu.VMEM((Z, 8, A), BF16),
        pltpu.VMEM((Y, X, B, A), BF16),
        pltpu.VMEM((Y, X, Z, 8, q), F32),
        pltpu.VMEM((Y // 2, R // Y, q), BF16),
        pltpu.VMEM((Y // 2, R // Y, q), BF16),
        dma((9,)),
        *[dma((C,)) for _ in range(12)],
        dma((X - 1,)), dma((X - 1,)),
        dma((Y - 1,)), dma((Y - 1,)),
        dma((2, Z // 2)), dma((2, Z // 2)),
        dma((3,)), dma((3,)),
        dma((Y // 2,)), dma((Y // 2,)),
    ]
    return pl.pallas_call(
        functools.partial(kernel, dims),
        out_shape=(
            jax.ShapeDtypeStruct((8, p), BF16),
            jax.ShapeDtypeStruct((R // 2, q), BF16),
        ),
        in_specs=[hbm] * 8,
        out_specs=(vmem, vmem),
        scratch_shapes=scratch,
        compiler_params=pltpu.CompilerParams(
            collective_id=0, has_side_effects=True, vmem_limit_bytes=50 * 1024 * 1024
        ),
        name="ladder_step",
    )(*[pltpu.with_memory_space_constraint(a, pltpu.HBM) for a in (mul, integ, amp, slab, slab_amp, rest, occupied, virtual)])


def solution(mesh, dims=(4, 4, 8)):
    placed = (
        P("op", "vp"),
        P("vp", None),
        P("op", "vp"),
        P("vp", "op"),
        P("vp", "op"),
        P("vp", "op"),
        P("op"),
        P("vp"),
    )
    return jax.shard_map(
        functools.partial(local, dims), mesh=mesh, in_specs=placed,
        out_specs=(P("vp", "op"), P("op", "vp")), check_vma=False,
    )
```

```python
import functools

import jax
import jax.numpy as jnp
from jax import lax
from jax.experimental import pallas as pl
from jax.experimental.pallas import tpu as pltpu
from jax.sharding import PartitionSpec as P

F32 = jnp.float32
BF16 = jnp.bfloat16
CHUNKS = 4


def kernel(
    dims,
    mul_hbm, int_hbm, amp_hbm, slab_hbm, slab_amp_hbm, rest_hbm, occ_hbm, virt_hbm,
    new_ref, den_ref,
    mul, integ, amp, slab, rest, occ, virt,
    lad, got1, sum1, got2, own3, sum2, got3, new_z, new_all, am_all, am_z, am_full, acc,
    swap_out, swap_in,
    load_sem, s1, r1, s2, r2, s3, r3, nz_s, nz_r, n2_s, n2_r, n3_s, n3_r,
    ax_s, ax_r, ay_s, ay_r, az_s, az_r, ag_s, ag_r, sw_s, sw_r,
):
    Y, X, Z = dims
    N = Y
    v = lax.axis_index("vp")
    c = lax.axis_index("op")
    y = v // (X * Z)
    x = lax.rem(v // Z, X)
    z = lax.rem(v, Z)
    B = 8 * Z
    R = X * B
    W = lad.shape[-1]
    chunks = lad.shape[0] // 2
    A = am_z.shape[-1]
    V = A // 2

    def near(axis, k):
        return lax.rem((y, x, z)[axis] + k, dims[axis])

    def at(axis, i):
        if axis == 0:
            return {"vp": (i * X + x) * Z + z}
        if axis == 1:
            return {"vp": (y * X + i) * Z + z}
        return {"vp": (y * X + x) * Z + i}

    other = {"op": 1 - c}

    def far_first(n):
        return sorted(range(1, n), key=lambda k: -min(k, n - k))

    sent = []

    def remote(src, dst, ss, rs, device):
        return pltpu.make_async_remote_copy(
            src_ref=src, dst_ref=dst, send_sem=ss, recv_sem=rs,
            device_id=device, device_id_type=pl.DeviceIdType.MESH,
        )

    def send(src, dst, ss, rs, device):
        d = remote(src, dst, ss, rs, device)
        d.start()
        sent.append(d)

    def arrived(ref, ss, rs, device):
        remote(ref, ref, ss, rs, device).wait_recv()

    def post(src, dst, ss, rs, device):
        remote(src, dst, ss, rs, device).start()

    def landed(bulk, ss, rs):
        remote(bulk, bulk, ss, rs, other).wait_recv()

    def left(bulk, ss, rs):
        remote(bulk, bulk, ss, rs, other).wait_send()

    loads = [
        pltpu.make_async_copy(src, dst, load_sem.at[i])
        for i, (src, dst) in enumerate([
            (slab_amp_hbm.at[:, pl.ds(A, mul.shape[0] - A)], am_all.at[z, y, x]),
            (int_hbm, integ), (mul_hbm, mul),
            (slab_amp_hbm.at[:, pl.ds(0, A)], am_z.at[z]),
            (slab_hbm, slab), (rest_hbm, rest), (occ_hbm, occ), (virt_hbm, virt), (amp_hbm, amp),
        ])
    ]
    for d in loads:
        d.start()

    barrier = pltpu.get_barrier_semaphore()
    greet = [at(a, near(a, k)) for a in range(3) for k in range(1, dims[a])] + [other]
    for device in greet:
        pl.semaphore_signal(barrier, inc=1, device_id=device, device_id_type=pl.DeviceIdType.MESH)
    def amp_own():
        mine = am_all.at[z, y, x]
        for k in range(1, X):
            send(mine, mine, ax_s.at[k - 1], ax_r.at[X - 1 - k], at(1, near(1, k)))

    def amp_rows():
        for i in range(X - 1):
            arrived(am_all.at[z, y, near(1, i + 1)], ax_s.at[i], ax_r.at[i], at(1, near(1, i + 1)))
        row = am_all.at[z, y]
        for k in range(1, Y):
            send(row, row, ay_s.at[k - 1], ay_r.at[Y - 1 - k], at(0, near(0, k)))

    H = Z // 2

    def ring_piece(side, step):
        block = near(2, Z - (step - 1)) if side == 0 else near(2, step - 1)
        if step < H:
            return am_all.at[block]
        return am_all.at[block, pl.ds(side * (Y // 2), Y // 2)]

    def ring_landed(side, step):
        block = near(2, Z - step) if side == 0 else near(2, step)
        if step < H:
            return am_all.at[block]
        return am_all.at[block, pl.ds(side * (Y // 2), Y // 2)]

    def ring_wait(step):
        for side in range(2):
            arrived(
                ring_landed(side, step), az_s.at[side, step - 1], az_r.at[side, step - 1],
                at(2, near(2, 1 if side == 0 else Z - 1)),
            )

    def ring_step(step):
        if step == 1:
            for i in range(Y - 1):
                arrived(am_all.at[z, near(0, i + 1)], ay_s.at[i], ay_r.at[i], at(0, near(0, i + 1)))
        else:
            ring_wait(step - 1)
        for side in range(2):
            piece = ring_piece(side, step)
            send(
                piece, piece, az_s.at[side, step - 1], az_r.at[side, step - 1],
                at(2, near(2, 1 if side == 0 else Z - 1)),
            )

    def axes(s):
        return (1, 0) if s % 2 == 0 else (0, 1)

    def ladder(part):
        streams = range(part * chunks, (part + 1) * chunks)
        lo = part * chunks * W
        for n in range(N):
            tile = lax.dot_general(
                integ[:, n * R:(n + 1) * R], mul[lo:lo + chunks * W, :],
                (((0,), (1,)), ((), ())), preferred_element_type=F32,
            )
            for s in streams:
                piece = tile[:, s * W - lo:(s + 1) * W - lo].astype(BF16).reshape(X, B, W)
                if s % 2 == 0:
                    lad[s, :, n] = piece
                else:
                    lad[s, n] = piece

    def ladder_send(chunk):
        for k in far_first(N):
            for s in (2 * chunk, 2 * chunk + 1):
                one = axes(s)[0]
                j = near(one, k)
                post(lad.at[s, j], got1.at[s, N - 1 - k], s1.at[chunk], r1.at[chunk], at(one, j))

    def ladder_next(chunk):
        left(got1.at[pl.ds(2 * chunk, 2)], s1.at[chunk], r1.at[chunk])
        ladder_send(chunk + 1)

    def sum_first(chunk):
        landed(got1.at[pl.ds(2 * chunk, 2)], s1.at[chunk], r1.at[chunk])
        for s in (2 * chunk + 1, 2 * chunk):
            one, two = axes(s)
            me = (y, x)[one]
            for k in far_first(N) + [N]:
                n = k - 1
                b = near(two, k)
                total = lad[s, me, b].astype(F32)
                for i in range(N - 1):
                    total = total + got1[s, i, b].astype(F32)
                if k < N:
                    sum1[s, n] = total.astype(BF16)
                    post(
                        sum1.at[s, n], got2.at[s, N - 1 - k], s2.at[chunk], r2.at[chunk], at(two, b)
                    )
                else:
                    own3[chunk, :, (s % 2) * W:(s % 2 + 1) * W] = total

    def sum_second(chunk):
        landed(got2.at[pl.ds(2 * chunk, 2)], s2.at[chunk], r2.at[chunk])
        for o in range(2):
            s = 2 * chunk + o
            two = axes(s)[1]
            cols = slice(o * W, (o + 1) * W)
            total = own3[chunk, :, cols]
            for i in range(N - 1):
                total = total + got2[s, i].astype(F32)
            own3[chunk, :, cols] = total
            sum2[chunk, :, :, cols] = total.reshape(Z, 8, W).astype(BF16)
        for k in far_first(Z):
            zb = near(2, k)
            post(
                sum2.at[chunk, zb], got3.at[chunk, Z - 1 - k], s3.at[chunk], r3.at[chunk], at(2, zb)
            )

    def renew(chunk):
        cols = slice(chunk * 2 * W, (chunk + 1) * 2 * W)
        landed(got3.at[chunk], s3.at[chunk], r3.at[chunk])
        total = own3[chunk, pl.ds(pl.multiple_of(z * 8, 8), 8), :]
        for i in range(Z - 1):
            total = total + got3[chunk, i].astype(F32)
        row = lax.broadcasted_iota(jnp.int32, (8, 8), 0)
        col = lax.broadcasted_iota(jnp.int32, (8, 8), 1)
        energy = jnp.broadcast_to(virt[...].astype(F32).reshape(1, 8), (8, 8))
        energy = jnp.sum(jnp.where(row == col, energy, 0.0), axis=1, keepdims=True)
        divisor = energy - occ[cols].astype(F32).reshape(1, 2 * W)
        renewed = slab[:, cols].astype(F32) + (total + rest[:, cols].astype(F32)) / divisor
        renewed = renewed.astype(BF16)
        new_ref[:, cols] = renewed
        new_z[chunk, z] = renewed
        here = new_z.at[chunk, z]
        for k in far_first(Z):
            post(here, here, nz_s.at[chunk], nz_r.at[chunk], at(2, near(2, k)))

    def spread_own(chunk):
        landed(got3.at[chunk], nz_s.at[chunk], nz_r.at[chunk])
        whole = new_z[chunk].astype(F32).reshape(B, 2 * W).astype(BF16)
        new_all[y, x, :, chunk * 2 * W:(chunk + 1) * 2 * W] = whole
        for k in far_first(N):
            for s in (2 * chunk, 2 * chunk + 1):
                two = axes(s)[1]
                here = new_all.at[y, x, :, pl.ds(s * W, W)]
                post(here, here, n2_s.at[chunk], n2_r.at[chunk], at(two, near(two, k)))
        for k in far_first(N):
            for s in (2 * chunk, 2 * chunk + 1):
                one = axes(s)[0]
                here = new_all.at[y, x, :, pl.ds(s * W, W)]
                post(here, here, n3_s.at[chunk], n3_r.at[chunk], at(one, near(one, k)))

    def spread_got(chunk):
        landed(got2.at[pl.ds(2 * chunk, 2)], n2_s.at[chunk], n2_r.at[chunk])
        for k in far_first(N):
            for i in far_first(N):
                for s in (2 * chunk, 2 * chunk + 1):
                    one, two = axes(s)
                    cols = pl.ds(s * W, W)
                    b = near(two, i)
                    here = new_all.at[b, x, :, cols] if s % 2 == 0 else new_all.at[y, b, :, cols]
                    post(here, here, n3_s.at[chunk], n3_r.at[chunk], at(one, near(one, k)))

    def spread_wait(chunk):
        landed(got1.at[pl.ds(2 * chunk, 2)], n3_s.at[chunk], n3_r.at[chunk])

    def all_left(chunk):
        pair = pl.ds(2 * chunk, 2)
        if chunk == chunks - 1:
            left(got1.at[pair], s1.at[chunk], r1.at[chunk])
        left(got2.at[pair], s2.at[chunk], r2.at[chunk])
        left(got3.at[chunk], s3.at[chunk], r3.at[chunk])
        left(got3.at[chunk], nz_s.at[chunk], nz_r.at[chunk])
        left(got2.at[pair], n2_s.at[chunk], n2_r.at[chunk])

    def staged_z():
        here = am_z.at[z]
        for k in far_first(Z):
            post(here, here, ag_s.at[0], ag_r.at[0], at(2, near(2, k)))

    def staged_own():
        landed(am_z.at[pl.ds(0, Z - 1)], ag_s.at[0], ag_r.at[0])
        am_full[y, x] = am_z[...].astype(F32).reshape(B, A).astype(BF16)
        for k in range(1, N):
            for o in range(2):
                here = am_full.at[y, x, :, pl.ds(o * V, V)]
                post(here, here, ag_s.at[1], ag_r.at[1], at(axes(o)[1], near(axes(o)[1], k)))

    def staged_got():
        landed(am_full.at[0, pl.ds(0, N - 1)], ag_s.at[1], ag_r.at[1])
        for k in range(1, N):
            for o in range(2):
                cols = pl.ds(o * V, V)
                here = am_full.at[:, x, :, cols] if o == 0 else am_full.at[y, :, :, cols]
                post(here, here, ag_s.at[2], ag_r.at[2], at(axes(o)[0], near(axes(o)[0], k)))

    def staged_wait():
        landed(am_full.at[pl.ds(0, N - 1)], ag_s.at[2], ag_r.at[2])
        left(am_z.at[pl.ds(0, Z - 1)], ag_s.at[0], ag_r.at[0])
        left(am_full.at[0, pl.ds(0, N - 1)], ag_s.at[1], ag_r.at[1])
        left(am_full.at[pl.ds(0, N - 1)], ag_s.at[2], ag_r.at[2])

    def amp_part(zb):
        rows = am_all[zb].astype(F32).reshape(Y * X * 8, mul.shape[0] - A).astype(BF16)
        acc[:, :, zb] = jnp.dot(rows, mul[A:, :], preferred_element_type=F32).reshape(Y, X, 8, acc.shape[-1])

    K = mul.shape[0] // 2

    def product(half, yb):
        left = new_all[yb, :, :, half * K:(half + 1) * K].reshape(R, K)
        return jnp.dot(left, amp[half * K:(half + 1) * K, :], preferred_element_type=F32)

    loads[1].wait()
    loads[2].wait()
    ladder(0)
    loads[0].wait()
    loads[3].wait()
    pl.semaphore_wait(barrier, len(greet))
    amp_own()
    staged_z()
    ladder_send(0)
    ladder(1)
    ladder_next(0)
    amp_rows()
    for d in loads[4:]:
        d.wait()
    sum_first(0)
    ladder_next(1)
    sum_first(1)
    ladder_next(2)
    staged_own()
    ring_step(1)
    sum_second(0)
    sum_first(2)
    sum_second(1)
    sum_first(3)
    renew(0)
    sum_second(2)
    staged_got()
    ring_step(2)
    renew(1)
    sum_second(3)
    spread_own(0)
    renew(2)
    ring_step(3)
    spread_own(1)
    renew(3)
    spread_got(0)
    spread_own(2)
    spread_got(1)
    ring_step(4)
    spread_own(3)
    spread_got(2)
    spread_got(3)
    amp_part(z)
    for k in range(1, H):
        amp_part(near(2, k))
        amp_part(near(2, Z - k))
    ring_wait(4)
    amp_part(near(2, H))
    staged_wait()
    for chunk in range(chunks):
        all_left(chunk)
    for chunk in range(chunks // 2):
        spread_wait(chunk)

    @pl.loop(0, Y)
    def _(t):
        staged = jnp.dot(am_full[t].reshape(R, A), mul[:A, :], preferred_element_type=F32)
        acc[t] = acc[t] + (product(0, t) + staged).reshape(acc.shape[1:])

    for chunk in range(chunks // 2, chunks):
        spread_wait(chunk)
    swaps = []
    half = X // 2
    D = half * B

    def final_rows(core, t):
        yb = core * (Y // 2) + t // 2
        xs = slice((t % 2) * half, (t % 2 + 1) * half)
        left_rows = new_all[yb, xs, :, K:].reshape(D, K)
        return acc[yb, xs].reshape(D, acc.shape[-1]) + jnp.dot(
            left_rows, amp[K:, :], preferred_element_type=F32
        )

    for t in range(Y):
        swap_out[t] = final_rows(1 - c, t).astype(BF16)
        d = remote(swap_out.at[t], swap_in.at[t], sw_s.at[t], sw_r.at[t], other)
        d.start()
        swaps.append(d)
    for t in range(Y):
        mine_t = final_rows(c, t)
        swaps[t].wait_recv()
        den_ref[pl.ds(t * D, D), :] = (mine_t + swap_in[t].astype(F32)).astype(BF16)
    for chunk in range(chunks):
        left(got1.at[pl.ds(2 * chunk, 2)], n3_s.at[chunk], n3_r.at[chunk])
    for d in sent + swaps:
        d.wait_send()


def local(dims, mul, integ, amp, slab, slab_amp, rest, occupied, virtual):
    Y, X, Z = dims
    N = Y
    B = 8 * Z
    R = Y * X * B
    C = CHUNKS
    S = 2 * C
    p, q = mul.shape
    W = p // S
    A = p // 2
    dma = pltpu.SemaphoreType.DMA
    vmem = pl.BlockSpec(memory_space=pltpu.VMEM)
    hbm = pl.BlockSpec(memory_space=pltpu.HBM)
    scratch = [
        pltpu.VMEM((p, q), BF16),
        pltpu.VMEM((q, R), BF16),
        pltpu.VMEM((p, q), BF16),
        pltpu.VMEM((8, p), BF16),
        pltpu.VMEM((8, p), BF16),
        pltpu.VMEM((p,), BF16),
        pltpu.VMEM((8,), BF16),
        pltpu.VMEM((S, Y, X, B, W), BF16),
        pltpu.VMEM((S, N - 1, N, B, W), BF16),
        pltpu.VMEM((S, N - 1, B, W), BF16),
        pltpu.VMEM((S, N - 1, B, W), BF16),
        pltpu.VMEM((C, B, 2 * W), F32),
        pltpu.VMEM((C, Z, 8, 2 * W), BF16),
        pltpu.VMEM((C, Z - 1, 8, 2 * W), BF16),
        pltpu.VMEM((C, Z, 8, 2 * W), BF16),
        pltpu.VMEM((Y, X, B, p), BF16),
        pltpu.VMEM((Z, Y, X, 8, p - A), BF16),
        pltpu.VMEM((Z, 8, A), BF16),
        pltpu.VMEM((Y, X, B, A), BF16),
        pltpu.VMEM((Y, X, Z, 8, q), F32),
        pltpu.VMEM((Y, R // Y // 2, q), BF16),
        pltpu.VMEM((Y, R // Y // 2, q), BF16),
        dma((9,)),
        *[dma((C,)) for _ in range(12)],
        dma((X - 1,)), dma((X - 1,)),
        dma((Y - 1,)), dma((Y - 1,)),
        dma((2, Z // 2)), dma((2, Z // 2)),
        dma((3,)), dma((3,)),
        dma((Y,)), dma((Y,)),
    ]
    return pl.pallas_call(
        functools.partial(kernel, dims),
        out_shape=(
            jax.ShapeDtypeStruct((8, p), BF16),
            jax.ShapeDtypeStruct((R // 2, q), BF16),
        ),
        in_specs=[hbm] * 8,
        out_specs=(vmem, vmem),
        scratch_shapes=scratch,
        compiler_params=pltpu.CompilerParams(
            collective_id=0, has_side_effects=True, vmem_limit_bytes=50 * 1024 * 1024
        ),
        name="ladder_step",
    )(*[pltpu.with_memory_space_constraint(a, pltpu.HBM) for a in (mul, integ, amp, slab, slab_amp, rest, occupied, virtual)])


def solution(mesh, dims=(4, 4, 8)):
    placed = (
        P("op", "vp"),
        P("vp", None),
        P("op", "vp"),
        P("vp", "op"),
        P("vp", "op"),
        P("vp", "op"),
        P("op"),
        P("vp"),
    )
    return jax.shard_map(
        functools.partial(local, dims), mesh=mesh, in_specs=placed,
        out_specs=(P("vp", "op"), P("op", "vp")), check_vma=False,
    )
```
